32 devices in a mesh: prow: 4 (over x, core), pcol: 8 (over z, y).
Axes of the slice: x: 2, y: 2, z: 4, core: 2. Of those that a mesh axis runs over, the one named last changes fastest.
Arguments:
- child_u: bfloat16 [2, 10, 4, 2, 8, 512, 128], P(None, None, 'prow', None, 'pcol'), may hold values from -5 to 5
- child_v: bfloat16 [2, 10, 4, 2, 8, 512, 128], P(None, None, 'prow', None, 'pcol'), may hold values from -5 to 5
- child_rank: int32 [2, 10, 4, 2, 8], P(None, None, 'prow', None, 'pcol'), may hold values from 0 to 128, as said below
- diag_shift: float32 [16, 512], replicated, may hold values from 0.5 to 4
Outputs:
- front_out: float32 [10, 4, 512, 2, 8, 512], P(None, 'prow', None, None, 'pcol')
The draws below stay inside these ranges and needn't reach their ends.
Inputs may be any that keep to these rules, and one draw needn't show every extreme that they name: `child_rank`: 0 on and above the block diagonal (i <= j); below it 0 where the child has no tile, else from 16 to 128.
All inputs are finite; a program needn't handle non-finite values.
Results may differ from the reference program's by a relative error of at most 0.0003.
Values may be sent and summed in bfloat16 or wider, within the bound.
A program may use at most 320 MiB of HBM per device.

```python
import math
import jax
import jax.numpy as jnp
from jax import lax

BLOCK = 512
RANK_MAX = 128
CHILDREN = 2
PANELS = 2
NBLK = 40
SLAB = 16
N_PROW = 4
N_PCOL = 8


def draw_child_rank(key, part):
    key_rank = jax.random.fold_in(key, 11)
    key_keep = jax.random.fold_in(key, 23)
    shape = (CHILDREN, NBLK // N_PROW, N_PROW, SLAB // N_PCOL, N_PCOL)
    block_rows = lax.broadcasted_iota(jnp.int32, shape, 1) * N_PROW + lax.broadcasted_iota(jnp.int32, shape, 2)
    block_cols = lax.broadcasted_iota(jnp.int32, shape, 3) * N_PCOL + lax.broadcasted_iota(jnp.int32, shape, 4)
    ranks = jax.random.randint(key_rank, shape, RANK_MAX // 8, RANK_MAX + 1)
    present = jax.random.randint(key_keep, shape, 0, 4) > 0
    return jnp.where((block_rows > block_cols) & present, ranks, 0).astype(jnp.int32)


def block_levels(key, dims, split, smallest, top_value):
    loudness, own = 1.0, jax.random.fold_in(key, 6)
    for position, blocks in split:
        steps = jnp.exp(jax.random.uniform(jax.random.fold_in(own, position), (blocks,), jnp.float32, smallest / len(split), top_value / len(split)))
        loudness = loudness * jnp.repeat(steps, dims[position] // blocks).reshape([-1 if axis == position else 1 for axis in range(len(dims))])
    return loudness


def scatter_about(key, shape, deviation, limit, pieces=(), kind=jnp.bfloat16):
    array = deviation * jax.random.normal(key, shape, jnp.float32)
    if pieces:
        array = array * block_levels(key, shape, pieces, -0.22, 0.18)
    return jnp.clip(array, -limit, limit).astype(kind)


def setup_inputs(seed: int = 0) -> dict:
    splits = jax.random.split(jax.random.key(seed), 5)
    child_u = scatter_about(splits[0], (CHILDREN, NBLK // N_PROW, N_PROW, SLAB // N_PCOL, N_PCOL, BLOCK, RANK_MAX), 0.35, 5.0, ((2, 4), (4, 8)))
    child_v = scatter_about(splits[1], (CHILDREN, NBLK // N_PROW, N_PROW, SLAB // N_PCOL, N_PCOL, BLOCK, RANK_MAX), 0.35, 5.0, ((2, 4), (4, 8)))
    child_rank = draw_child_rank(jax.random.fold_in(splits[4], 71), 0)
    diag_shift = jnp.clip(jnp.exp(jax.random.uniform(splits[3], (SLAB, BLOCK), jnp.float32, math.log(0.5), math.log(4.0))), 0.5, 4.0)
    return {"child_u": child_u, "child_v": child_v, "child_rank": child_rank, "diag_shift": diag_shift}


def reference(child_u, child_v, child_rank, diag_shift):
    precise = lax.Precision.HIGHEST
    rank_grid = child_rank.reshape(CHILDREN, NBLK, SLAB)
    keep_mask = (jnp.arange(RANK_MAX, dtype=jnp.int32)[None, None, None, :] < rank_grid[:, :, :, None]).astype(jnp.bfloat16)
    left_factor = child_u.reshape(CHILDREN, NBLK, SLAB, BLOCK, RANK_MAX) * keep_mask[:, :, :, None, :]
    right_factor = child_v.reshape(CHILDREN, NBLK, SLAB, BLOCK, RANK_MAX) * keep_mask[:, :, :, None, :]
    left_cols = left_factor.transpose(2, 0, 1, 3, 4)
    right_cols = right_factor.transpose(2, 0, 1, 3, 4)

    def assemble(operands):
        left_part = operands[0].astype(jnp.float32)
        right_part = operands[1].astype(jnp.float32)
        tile_col = jnp.einsum('ciak,cibk->iab', left_part, right_part, precision=precise)
        column_sum = jnp.einsum('ciak,cibk->ab', right_part, right_part, precision=precise)
        return (tile_col, column_sum)
    front_cols, column_sums = lax.map(assemble, (left_cols, right_cols))

    def row_part(row_factor):
        row_factor = row_factor.astype(jnp.float32)
        return jnp.einsum('cjak,cjbk->ab', row_factor, row_factor, precision=precise)
    row_sums = lax.map(row_part, left_factor.transpose(1, 0, 2, 3, 4)[:SLAB])
    diagonal_index = jnp.arange(SLAB, dtype=jnp.int32)
    identity = jnp.eye(BLOCK, dtype=jnp.float32)
    diag_terms = row_sums + column_sums + identity[None] * diag_shift[:, None, :]
    front_cols = front_cols.at[diagonal_index, diagonal_index].add(diag_terms)
    block_rows = jnp.arange(NBLK, dtype=jnp.int32)
    panel_list = []
    for panel_index in range(PANELS):
        factor = jnp.linalg.cholesky(front_cols[panel_index, panel_index])
        solved = lax.linalg.triangular_solve(factor, front_cols[panel_index].reshape(NBLK * BLOCK, BLOCK), left_side=False, lower=True, transpose_a=True).reshape(NBLK, BLOCK, BLOCK)
        below_mask = (block_rows > panel_index)[:, None, None]
        solved = jnp.where(below_mask, solved, 0.0)
        pivot_diag = jnp.diagonal(factor)
        at_pivot = (block_rows == panel_index)[:, None, None]
        panel_list.append(jnp.where(at_pivot, (factor * pivot_diag[None, :])[None], solved * pivot_diag[None, None, :]))
        rounded = lax.optimization_barrier(solved.astype(jnp.bfloat16)).astype(jnp.float32)

        def update(operands, rounded=rounded):
            return operands[0] - jnp.einsum('iab,cb->iac', rounded, operands[1], precision=precise)
        front_cols = lax.map(update, (front_cols, rounded[:SLAB]))
    slab_index = jnp.arange(SLAB, dtype=jnp.int32)
    lower_mask = (block_rows[None, :] >= slab_index[:, None])[:, :, None, None]
    final = jnp.where(lower_mask, front_cols, 0.0)
    final = final.at[:PANELS].set(jnp.stack(panel_list))
    final = final.reshape(SLAB // N_PCOL, N_PCOL, NBLK // N_PROW, N_PROW, BLOCK, BLOCK).transpose(2, 3, 4, 0, 1, 5)
    return final
```

```python
import functools

import jax
import jax.numpy as jnp
from jax import lax
from jax.experimental import pallas as pl
from jax.experimental.pallas import tpu as pltpu
from jax.sharding import PartitionSpec as P

PANELS = 2
STEP = 128
SUB = 8


def nt(a, b, precision=None):
    return lax.dot_general(
        a, b, (((1,), (1,)), ((), ())), preferred_element_type=jnp.float32, precision=precision
    )


def nn(a, b, precision=None):
    return lax.dot_general(
        a, b, (((1,), (0,)), ((), ())), preferred_element_type=jnp.float32, precision=precision
    )


def factor_kernel(s_ref, c_ref, y_ref, w_ref, e_ref):
    extent = s_ref.shape[0]
    exact = lax.Precision.HIGHEST
    w_ref[...] = s_ref[...]
    e_ref[...] = (
        lax.broadcasted_iota(jnp.int32, (extent, extent), 0)
        == lax.broadcasted_iota(jnp.int32, (extent, extent), 1)
    ).astype(jnp.float32)
    groups = STEP // SUB
    sub_row = lax.broadcasted_iota(jnp.int32, (SUB, STEP), 0)
    lane = lax.broadcasted_iota(jnp.int32, (SUB, STEP), 1)

    @pl.loop(0, extent // STEP)
    def _(block):
        base = pl.multiple_of(block * STEP, STEP)
        here = pl.ds(base, STEP)
        tile = w_ref[here, here]
        left = [tile[g * SUB : (g + 1) * SUB] for g in range(groups)]
        right = [(lane == sub_row + g * SUB).astype(jnp.float32) for g in range(groups)]
        for j in range(STEP):
            own, inner = divmod(j, SUB)
            row = left[own][inner : inner + 1]
            inverse = 1.0 / jnp.broadcast_to(row[:, j : j + 1], (1, STEP))
            row_left = jnp.broadcast_to(row * inverse, (SUB, STEP))
            row_right = jnp.broadcast_to(right[own][inner : inner + 1] * inverse, (SUB, STEP))
            for g in range(own, groups):
                weight = jnp.broadcast_to(left[g][:, j : j + 1], (SUB, STEP))
                if g == own:
                    weight = jnp.where(sub_row > inner, weight, 0.0)
                left[g] = left[g] - weight * row_left
                right[g] = right[g] - weight * row_right
        upper = jnp.concatenate(left, axis=0)
        lower_inverse = jnp.concatenate(right, axis=0)
        tile_row = lax.broadcasted_iota(jnp.int32, (STEP, STEP), 0)
        tile_col = lax.broadcasted_iota(jnp.int32, (STEP, STEP), 1)
        pivots = jnp.sum(jnp.where(tile_row == tile_col, upper, 0.0), axis=1, keepdims=True)
        root = jnp.sqrt(pivots)
        pivot_factor = (jnp.where(tile_row <= tile_col, upper, 0.0) / root).T
        pivot_inverse = lower_inverse / root
        panel = nt(w_ref[:, here], pivot_inverse, exact)
        below = lax.broadcasted_iota(jnp.int32, (extent, STEP), 0) >= base + STEP
        panel = jnp.where(below, panel, 0.0)
        c_ref[:, here] = panel
        c_ref[here, here] = pivot_factor
        solved = nn(pivot_inverse, e_ref[here, :], exact)
        y_ref[here, :] = solved
        w_ref[...] -= nt(panel, panel, exact)
        e_ref[...] -= nn(panel, solved, exact)


def factor(pivot_tile):
    shape = jax.ShapeDtypeStruct(pivot_tile.shape, jnp.float32)
    spec = pl.BlockSpec(memory_space=pltpu.VMEM)
    return pl.pallas_call(
        factor_kernel,
        out_shape=(shape, shape),
        in_specs=[spec],
        out_specs=(spec, spec),
        scratch_shapes=[pltpu.VMEM(pivot_tile.shape, jnp.float32)] * 2,
        compiler_params=pltpu.CompilerParams(vmem_limit_bytes=24 * 2**20),
        cost_estimate=pl.CostEstimate(
            flops=60_000_000_000, bytes_accessed=3 * 2**20, transcendentals=0
        ),
        name="factor",
    )(pivot_tile)


def finish_kernel(prow_count, pcol_count, at_ref, u_ref, v_ref, g_ref, h_ref, d_ref, p_ref, o_ref):
    t, r = pl.program_id(0), pl.program_id(1)
    i = r * prow_count + at_ref[0]
    j = t * pcol_count + at_ref[1]

    @pl.when(i < j)
    def _():
        o_ref[0] = jnp.zeros_like(o_ref[0])

    @pl.when((i >= j) & (j < PANELS))
    def _():
        o_ref[0] = p_ref[0]

    @pl.when((i >= j) & (j >= PANELS))
    def _():
        total = -nt(g_ref[0], h_ref[0])
        for c in range(u_ref.shape[0]):
            total += nt(u_ref[c, 0, 0], v_ref[c, 0, 0])
        o_ref[0] = total

    @pl.when((i == j) & (j >= PANELS))
    def _():
        o_ref[0] += d_ref[0]


def finish(prow_count, pcol_count, at, left, right, solved, other, diag, panels):
    children, rows, cols, extent, rank = left.shape
    wide = solved.shape[-1]
    factor_spec = pl.BlockSpec((children, 1, 1, extent, rank), lambda t, r, at: (0, r, t, 0, 0))
    return pl.pallas_call(
        functools.partial(finish_kernel, prow_count, pcol_count),
        out_shape=jax.ShapeDtypeStruct((rows, extent, cols * extent), jnp.float32),
        grid_spec=pltpu.PrefetchScalarGridSpec(
            num_scalar_prefetch=1,
            grid=(cols, rows),
            in_specs=[
                factor_spec,
                factor_spec,
                pl.BlockSpec((1, extent, wide), lambda t, r, at: (r, 0, 0)),
                pl.BlockSpec((1, extent, wide), lambda t, r, at: (t, 0, 0)),
                pl.BlockSpec((1, extent, extent), lambda t, r, at: (t, 0, 0)),
                pl.BlockSpec(
                    (1, extent, extent), lambda t, r, at: (jnp.where(t == 0, r, rows - 1), 0, 0)
                ),
            ],
            out_specs=pl.BlockSpec((1, extent, extent), lambda t, r, at: (r, 0, t)),
        ),
        compiler_params=pltpu.CompilerParams(vmem_limit_bytes=48 * 2**20),
        cost_estimate=pl.CostEstimate(
            flops=2 * rows * cols * extent * extent * (wide + children * rank),
            bytes_accessed=60 * 2**20,
            transcendentals=0,
        ),
        name="finish",
    )(at, left, right, solved, other, diag, panels)


def pieces(value, count):
    parts = []
    for _ in range(count):
        part = lax.reduce_precision(value, 8, 7)
        parts.append(part.astype(jnp.bfloat16))
        value = value - part
    return parts


def times(left_parts, right_parts, pattern):
    total = None
    for a in left_parts:
        for b in right_parts:
            term = jnp.einsum(pattern, a, b, preferred_element_type=jnp.float32)
            total = term if total is None else total + term
    return total


def on_device(child_u, child_v, child_rank, diag_shift):
    prow_count = lax.axis_size("prow")
    pcol_count = lax.axis_size("pcol")
    own_row = lax.axis_index("prow")
    own_column = lax.axis_index("pcol")
    both = ("prow", "pcol")
    rank_grid = child_rank[:, :, 0, :, 0]
    rows_here = rank_grid.shape[1]
    cols_here = rank_grid.shape[2]
    extent = child_u.shape[-2]
    keep_mask = (
        jnp.arange(child_u.shape[-1], dtype=jnp.int32)[None, None, None, :]
        < rank_grid[:, :, :, None]
    ).astype(jnp.bfloat16)
    left = child_u[:, :, 0, :, 0] * keep_mask[:, :, :, None, :]
    right = child_v[:, :, 0, :, 0] * keep_mask[:, :, :, None, :]
    kept_rows = cols_here * pcol_count // prow_count
    row_terms = jnp.einsum(
        "crtak,crtbk->rab", left[:, :kept_rows], left[:, :kept_rows],
        preferred_element_type=jnp.float32,
    )
    column_terms = [
        jnp.einsum(
            "crak,crbk->ab", right[:, :, t], right[:, :, t], preferred_element_type=jnp.float32
        )
        for t in range(cols_here)
    ]
    zero = jnp.zeros((extent, extent), jnp.float32)
    pivot_parts = []
    for k in range(PANELS):
        row, col = k // prow_count, k // pcol_count
        in_row = own_row == k % prow_count
        in_col = own_column == k % pcol_count
        part = jnp.where(in_col, column_terms[col], zero)
        part = part + jnp.where(in_row, row_terms[row], zero)
        own_tile = jnp.einsum(
            "cak,cbk->ab", left[:, row, col], right[:, row, col],
            preferred_element_type=jnp.float32,
        )
        pivot_parts.append(part + jnp.where(in_row & in_col, own_tile, zero))
    pivot_sums = lax.psum(jnp.stack(pivot_parts), both)

    pairs = [(m, k) for k in range(PANELS) for m in range(k + 1, PANELS)]
    pair_factors = []
    for m, k in pairs:
        root = (own_row == m % prow_count) & (own_column == k % pcol_count)
        tile = jnp.stack(
            [f[:, m // prow_count, k // pcol_count] for f in (left, right)]
        )
        pair_factors.append(jnp.where(root, tile, jnp.zeros_like(tile)))
    pair_factors = lax.psum(jnp.stack(pair_factors), both)

    panel_factors = []
    for k in range(PANELS):
        tiles = jnp.stack([f[:, :, k // pcol_count] for f in (left, right)])
        panel_factors.append(
            jnp.where(own_column == k % pcol_count, tiles, jnp.zeros_like(tiles))
        )
    panel_factors = lax.psum(jnp.stack(panel_factors), "pcol")

    block_rows = jnp.arange(rows_here, dtype=jnp.int32) * prow_count + own_row
    block_cols = jnp.arange(cols_here, dtype=jnp.int32) * pcol_count + own_column
    other_factors = jnp.take(panel_factors, block_cols // prow_count, axis=3)
    other_factors = lax.psum(
        jnp.where(own_row == own_column % prow_count, other_factors, jnp.zeros_like(other_factors)),
        "prow",
    )
    row_sums = lax.psum(row_terms, "pcol")
    column_sums = lax.psum(jnp.stack(column_terms), "prow")

    identity = jnp.eye(extent, dtype=jnp.float32)
    near_rows = jnp.concatenate([block_rows, block_cols])
    near_factors = jnp.concatenate([panel_factors, other_factors], axis=3)
    rounded = []
    fixed = {m: [] for m in range(PANELS)}
    panels = jnp.zeros((rows_here, extent, extent), jnp.float32)
    for k in range(PANELS):
        pivot_tile = pivot_sums[k] + identity * diag_shift[k][None, :]
        for g in fixed[k]:
            pivot_tile = pivot_tile - nt(g, g)
        lower, inverse = factor(pivot_tile)
        inverse_parts = pieces(inverse, 3)
        carried = [pieces(times(inverse_parts, [g], "ab,bk->ak"), 2) for g in fixed[k]]

        def solve(left_tiles, right_tiles, earlier):
            moved = times(inverse_parts, [right_tiles], "ab,crbk->crak")
            value = times([left_tiles], pieces(moved, 2), "crak,crbk->rab")
            for g, parts in zip(earlier, carried):
                value = value - times([g], parts, "rak,bk->rab")
            return value

        for position, (m, kk) in enumerate(pairs):
            if kk == k:
                tile = pair_factors[position]
                earlier = [g[None] for g in fixed[m]]
                value = solve(tile[0][:, None], tile[1][:, None], earlier)
                fixed[m].append(value[0].astype(jnp.bfloat16))
        value = solve(near_factors[k, 0], near_factors[k, 1], rounded)
        value = jnp.where((near_rows > k)[:, None, None], value, 0.0)
        rounded.append(value.astype(jnp.bfloat16))
        scale = jnp.diagonal(lower)
        panel = jnp.where(
            (block_rows == k)[:, None, None], lower[None], value[:rows_here]
        ) * scale[None, None, :]
        panels = jnp.where(own_column == k % pcol_count, panel, panels)

    wide = jnp.concatenate(rounded, axis=-1)
    select_cols = (
        block_cols[:, None] == jnp.arange(diag_shift.shape[0], dtype=jnp.int32)[None, :]
    ).astype(jnp.float32)
    shift_cols = jnp.dot(select_cols, diag_shift, precision=lax.Precision.HIGHEST)
    diag = (
        jnp.take(row_sums, block_cols // prow_count, axis=0)
        + column_sums
        + identity[None] * shift_cols[:, None, :]
    )
    at = jnp.stack([own_row, own_column]).astype(jnp.int32)
    out = finish(
        prow_count, pcol_count, at, left, right, wide[:rows_here], wide[rows_here:], diag, panels
    )
    return out.reshape(rows_here, 1, extent, cols_here, 1, extent)


def solution(mesh):
    placed = (
        P(None, None, "prow", None, "pcol", None, None),
        P(None, None, "prow", None, "pcol", None, None),
        P(None, None, "prow", None, "pcol"),
        P(),
    )
    return jax.shard_map(
        on_device,
        mesh=mesh,
        in_specs=placed,
        out_specs=P(None, "prow", None, None, "pcol", None),
        check_vma=False,
    )
```
